32 devices in a mesh: groups: 2 (over y), expert: 4 (over z), dp: 2 (over x), tile: 2 (over core).
Axes of the slice: x: 2, y: 2, z: 4, core: 2. Of those that a mesh axis runs over, the one named last changes fastest.
Arguments:
- features: bfloat16 [256, 1024], P(('groups', 'expert', 'dp', 'tile')), parts along dimension 0, may hold values from -6 to 6
- cross_weight: bfloat16 [1024, 1024], P(None, ('dp', 'tile')), may hold values from -0.1875 to 0.1875
- cross_bias: float32 [1024], replicated, may hold values from -1 to 1
- gate_weight: bfloat16 [1024, 36], replicated, may hold values from -24 to 24
- unit_experts: int32 [6, 6], replicated, may hold values from 0 to 15, all different within a row
- up_weight: bfloat16 [1024, 65536], P(None, ('expert', 'dp')), may hold values from -0.1875 to 0.1875
- up_bias: float32 [65536], P(('expert', 'dp')), may hold values from -3 to 3
- down_weight: bfloat16 [65536, 512], P(('expert', 'dp')), may hold values from -0.09375 to 0.09375
- down_bias: float32 [16, 512], replicated, may hold values from -3 to 3
- task_counts: int32 [32, 6], P(('groups', 'expert', 'dp', 'tile')), parts along dimension 0, may hold values from 1 to 8, as said below
- tower_in: bfloat16 [6, 512, 2048], P(None, None, ('dp', 'tile')), may hold values from -0.25 to 0.25
- tower_in_bias: float32 [6, 2048], P(None, ('dp', 'tile')), may hold values from -3 to 3
- tower_out: bfloat16 [6, 2048, 512], P(None, ('dp', 'tile')), may hold values from -0.125 to 0.125
- tower_out_bias: float32 [6, 512], replicated, may hold values from -3 to 3
Outputs:
- task_states: bfloat16 [256, 6, 512], P(('groups', 'expert', 'dp', 'tile')), parts along dimension 0
The draws below stay inside these ranges and needn't reach their ends.
There are 2 independent parts, one for each index of `groups`. The reference program is written for one: setup_inputs(seed, part) draws one part's arguments, and reference() takes and returns one part's arrays. A program takes and returns all parts, laid end to end along the dimension named above; an argument that names none is the same for every part. Nothing has to cross between parts.
Inputs may be any that keep to these rules, and one draw needn't show every extreme that they name: `task_counts`: every task reaches a count of 8 on some row shard; which one is drawn from the seed.
All inputs are finite; a program needn't handle non-finite values.
Results may differ from the reference program's by a relative error of at most 0.0095.
Values may be sent and summed in bfloat16 or wider, within the bound.
A program may use at most 64 MiB of HBM per device.

```python
import jax
import jax.numpy as jnp
from jax import lax

D = 1024
EXPERT_FF = 4096
OUT = 512
EXPERTS = 16
TASKS = 6
UNIT_K = 6
TFF = 2048
ROWS_DEV = 8
SHARDS = 16
ROWS = 128


def draw_gate_weight(key, part):
    values = 0.03 * jax.random.normal(jax.random.fold_in(key, 11), (D, TASKS * UNIT_K), jnp.float32)
    return jnp.clip(values, -24.0, 24.0).astype(jnp.bfloat16)


def draw_task_counts(key, part):
    draw_key, place_key = jax.random.split(jax.random.fold_in(key, 7))
    counts = jax.random.randint(draw_key, (SHARDS, TASKS), 1, ROWS_DEV + 1)
    fullest = jax.random.randint(place_key, (TASKS,), 0, SHARDS)
    full_marks = jnp.arange(SHARDS)[:, None] == fullest[None, :]
    return jnp.where(full_marks, ROWS_DEV, counts).astype(jnp.int32)


def block_levels(key, shape, pieces, low, largest):
    factor_of, own = 1.0, jax.random.fold_in(key, 6)
    for dim, blocks in pieces:
        draws = jnp.exp(jax.random.uniform(jax.random.fold_in(own, dim), (blocks,), jnp.float32, low / len(pieces), largest / len(pieces)))
        factor_of = factor_of * jnp.repeat(draws, shape[dim] // blocks).reshape([-1 if axis == dim else 1 for axis in range(len(shape))])
    return factor_of


def different_ones(stream_key, rows, count, top, lift):
    order = jax.random.permutation(jax.random.fold_in(stream_key, 1), count)
    boost = order
    for power in range(3):
        boost = boost * boost // count
    boost = boost * lift // count
    tickets = jax.random.randint(jax.random.fold_in(stream_key, 2), (rows, count), 0, 4096) + boost
    fixed_rows = jax.random.permutation(jax.random.fold_in(stream_key, 3), rows)[jnp.arange(count) % rows]
    tickets = jnp.where(jnp.arange(rows)[:, None] == fixed_rows[None, :], 1 << 14, tickets)
    priority = tickets * count + jnp.arange(count)
    return lax.top_k(priority.astype(jnp.int32), top)[1].astype(jnp.int32)


def centred(own_key, extent, scale, reach, pieces=(), kind=jnp.bfloat16):
    entries = scale * jax.random.normal(own_key, extent, jnp.float32)
    if pieces:
        entries = entries * block_levels(own_key, extent, pieces, -0.22, 0.18)
    return jnp.clip(entries, -reach, reach).astype(kind)


def setup_inputs(seed: int = 0, part: int = 0) -> dict:
    seeds = jax.random.split(jax.random.key(seed), 15)
    part_keys = jax.random.split(jax.random.fold_in(seeds[14], part), 15)
    features = centred(part_keys[0], (ROWS, D), 1.0, 6.0, ((0, 16),))
    cross_weight = centred(seeds[1], (D, D), D ** -0.5, 0.1875, ((1, 4),))
    cross_bias = jnp.clip(jax.random.uniform(seeds[2], (D,), jnp.float32, -1.0, 1.0), -1.0, 1.0)
    gate_weight = draw_gate_weight(jax.random.fold_in(seeds[14], 71), part)
    unit_experts = different_ones(seeds[4], TASKS, EXPERTS, UNIT_K, 0)
    up_weight = centred(seeds[5], (D, EXPERTS * EXPERT_FF), D ** -0.5, 0.1875, ((1, 8),))
    up_bias = centred(seeds[6], (EXPERTS * EXPERT_FF,), 0.5, 3.0, ((0, 8),), jnp.float32)
    down_weight = centred(seeds[7], (EXPERTS * EXPERT_FF, OUT), EXPERT_FF ** -0.5, 0.09375, ((0, 8),))
    down_bias = centred(seeds[8], (EXPERTS, OUT), 0.5, 3.0, (), jnp.float32)
    task_counts = draw_task_counts(jax.random.fold_in(jax.random.fold_in(seeds[14], part), 71), part)
    tower_in = centred(seeds[10], (TASKS, OUT, TFF), OUT ** -0.5, 0.25, ((2, 4),))
    tower_in_bias = centred(seeds[11], (TASKS, TFF), 0.5, 3.0, ((1, 4),), jnp.float32)
    tower_out = centred(seeds[12], (TASKS, TFF, OUT), TFF ** -0.5, 0.125, ((1, 4),))
    tower_out_bias = centred(seeds[13], (TASKS, OUT), 0.5, 3.0, (), jnp.float32)
    return {"features": features, "cross_weight": cross_weight, "cross_bias": cross_bias, "gate_weight": gate_weight, "unit_experts": unit_experts, "up_weight": up_weight, "up_bias": up_bias, "down_weight": down_weight, "down_bias": down_bias, "task_counts": task_counts, "tower_in": tower_in, "tower_in_bias": tower_in_bias, "tower_out": tower_out, "tower_out_bias": tower_out_bias}


def reference(features, cross_weight, cross_bias, gate_weight, unit_experts, up_weight, up_bias, down_weight, down_bias, task_counts, tower_in, tower_in_bias, tower_out, tower_out_bias):
    scaled = jnp.dot(features, cross_weight, preferred_element_type=jnp.float32) + cross_bias
    column_base = features.astype(jnp.float32)
    crossed = (column_base * scaled + column_base).astype(jnp.bfloat16)
    logits = jnp.dot(features, gate_weight, preferred_element_type=jnp.float32)
    gate_probs = jax.nn.softmax(logits.reshape(ROWS, TASKS, UNIT_K), axis=-1)

    def expert_block(expert_id):
        offset = (expert_id * EXPERT_FF).astype(jnp.int32)
        up_cols = lax.dynamic_slice_in_dim(up_weight, offset, EXPERT_FF, 1)
        bias_cols = lax.dynamic_slice_in_dim(up_bias, offset, EXPERT_FF, 0)
        down_rows = lax.dynamic_slice_in_dim(down_weight, offset, EXPERT_FF, 0)
        hidden = jax.nn.relu(jnp.dot(crossed, up_cols, preferred_element_type=jnp.float32) + bias_cols).astype(jnp.bfloat16)
        return jnp.dot(hidden, down_rows, preferred_element_type=jnp.float32)

    expert_out = lax.map(expert_block, jnp.arange(EXPERTS, dtype=jnp.int32)) + down_bias[:, None, :]
    onehot = (unit_experts[:, :, None] == jnp.arange(EXPERTS, dtype=jnp.int32)[None, None, :]).astype(jnp.float32)
    mix_weights = jnp.einsum("rtk,tke->rte", gate_probs, onehot)
    mixed_rows = jnp.einsum("rte,ero->rto", mix_weights, expert_out).astype(jnp.bfloat16)
    tower_hidden = jnp.einsum("rto,toh->rth", mixed_rows.astype(jnp.float32), tower_in.astype(jnp.float32))
    tower_hidden = jax.nn.relu(tower_hidden + tower_in_bias[None, :, :]).astype(jnp.bfloat16)
    tower_result = jnp.einsum("rth,tho->rto", tower_hidden.astype(jnp.float32), tower_out.astype(jnp.float32))
    tower_result = tower_result + tower_out_bias[None, :, :]
    row_ids = jnp.arange(ROWS, dtype=jnp.int32)
    shard_ids = row_ids // ROWS_DEV
    position = row_ids % ROWS_DEV
    active = position[:, None] < task_counts[shard_ids, :]
    return jnp.where(active[:, :, None], tower_result, 0.0).astype(jnp.bfloat16)
```

```python
import functools

import jax
import jax.numpy as jnp
from jax import lax
from jax.experimental import pallas as pl
from jax.experimental.pallas import tpu as pltpu
from jax.sharding import PartitionSpec as P

EXPERT_FF = 4096
MESH = pl.DeviceIdType.MESH
F32 = jnp.float32
BF16 = jnp.bfloat16


def kernel(
    sizes,
    features,
    cross_weight,
    cross_bias,
    gate_weight,
    unit_experts,
    up_weight,
    up_bias,
    down_weight,
    down_bias,
    task_counts,
    tower_in,
    tower_in_bias,
    tower_out,
    tower_out_bias,
    out,
    feats,
    cross_v,
    cross_b,
    gate_v,
    up_v,
    up_b,
    down_v,
    down_b,
    tin_v,
    tin_b,
    tout_v,
    tout_b,
    rows_all,
    acc,
    sent,
    parts,
    mix_w,
    mixed,
    tower_own,
    tower_send,
    tower_recv,
    local_sem,
    f_send,
    f_recv,
    c_send,
    c_fwd,
    c_recv,
    e_send,
    e_recv,
    m_send,
    m_recv,
    t_send,
    t_recv,
):
    planes, dp_size, tile_size = sizes
    plane_devs = dp_size * tile_size
    chips = planes * dp_size
    ranks = chips * tile_size
    z, x, c = lax.axis_index("expert"), lax.axis_index("dp"), lax.axis_index("tile")
    chip = z * dp_size + x
    me = chip * tile_size + c
    spot = x * tile_size + c
    own = features.shape[0]
    width = features.shape[1]
    cols = cross_weight.shape[1]
    plane_rows = own * plane_devs
    tasks, unit_k = unit_experts.shape
    experts, out_w = down_bias.shape
    hid = up_v.shape[1]
    hid_base = pl.multiple_of(c * hid, 128)

    def rank_id(q):
        return {
            "expert": q // plane_devs,
            "dp": (q // tile_size) % dp_size,
            "tile": q % tile_size,
        }

    def plane_id(g):
        return {"dp": g // tile_size, "tile": g % tile_size}

    def loop(n, fn):
        lax.fori_loop(0, n, lambda i, _: (fn(i), 0)[1], 0)

    barrier = pltpu.get_barrier_semaphore()

    def greet(i):
        q = lax.rem(me + 1 + i, ranks)
        pl.semaphore_signal(barrier, inc=1, device_id=rank_id(q), device_id_type=MESH)

    loop(ranks - 1, greet)

    half = width // 2
    moves = [
        pltpu.make_async_copy(src, dst, local_sem.at[i])
        for i, (src, dst) in enumerate(
            [
                (features, feats.at[spot]),
                (cross_weight, cross_v),
                (cross_bias, cross_b),
                (gate_weight, gate_v),
                (up_bias, up_b),
                (down_bias, down_b),
                (tower_in_bias, tin_b),
                (tower_out_bias, tout_b),
                (up_weight.at[pl.ds(0, half), pl.ds(hid_base, hid)], up_v.at[pl.ds(0, half)]),
                (
                    up_weight.at[pl.ds(half, half), pl.ds(hid_base, hid)],
                    up_v.at[pl.ds(half, half)],
                ),
                (down_weight.at[pl.ds(hid_base, hid), :], down_v),
                (tower_in, tin_v),
                (tower_out, tout_v),
            ]
        )
    ]
    for move in moves:
        move.start()
    pl.semaphore_wait(barrier, ranks - 1)

    def row_copy(src_spot, to):
        return pltpu.make_async_remote_copy(
            src_ref=features,
            dst_ref=feats.at[src_spot],
            send_sem=f_send.at[to],
            recv_sem=f_recv.at[src_spot],
            device_id=plane_id(to),
            device_id_type=MESH,
        )

    def other(i):
        return lax.rem(spot + 1 + i, plane_devs)

    loop(plane_devs - 1, lambda i: row_copy(spot, other(i)).start())
    for move in moves[:4]:
        move.wait()
    loop(plane_devs - 1, lambda i: row_copy(other(i), spot).wait_recv())

    col_base = pl.multiple_of(spot * cols, 128)
    rows_f = feats[...].astype(F32).reshape(plane_rows, width)
    scaled = jnp.dot(rows_f.astype(BF16), cross_v[...], preferred_element_type=F32)
    scaled = scaled + cross_b[:, pl.ds(col_base, cols)]
    base = feats[:, :, pl.ds(col_base, cols)].astype(F32).reshape(plane_rows, cols)

    def region(q):
        r0 = pl.multiple_of((q // plane_devs) * plane_rows, plane_rows)
        c0 = pl.multiple_of(lax.rem(q, plane_devs) * cols, 128)
        return rows_all.at[pl.ds(r0, plane_rows), pl.ds(c0, cols)]

    region(me)[...] = (base * scaled + base).astype(BF16)

    def block_copy(q, to, sem):
        return pltpu.make_async_remote_copy(
            src_ref=region(q),
            dst_ref=region(q),
            send_sem=sem,
            recv_sem=c_recv.at[q],
            device_id=rank_id(to),
            device_id_type=MESH,
        )

    def other_chip(i):
        return lax.rem(chip + 1 + i, chips)

    def chip_send(i):
        k = other_chip(i)
        return block_copy(me, k * tile_size + c, c_send.at[k])

    def forward(k, j):
        t = lax.rem(c + j, tile_size)
        return block_copy(k * tile_size + c, chip * tile_size + t, c_fwd.at[k, t])

    loop(chips - 1, lambda i: chip_send(i).start())
    for j in range(1, tile_size):
        forward(chip, j).start()

    logits = jnp.dot(feats[spot], gate_v[...], preferred_element_type=F32)
    lane = lax.broadcasted_iota(jnp.int32, logits.shape, 1)
    probs = jnp.zeros_like(logits)
    picks = jnp.full(logits.shape, -1, jnp.int32)
    for t in range(tasks):
        group = (lane >= t * unit_k) & (lane < (t + 1) * unit_k)
        top = jnp.max(jnp.where(group, logits, -jnp.inf), axis=1, keepdims=True)
        powers = jnp.where(group, jnp.exp(jnp.where(group, logits - top, 0.0)), 0.0)
        probs = probs + powers / jnp.sum(powers, axis=1, keepdims=True)
        for k in range(unit_k):
            picks = jnp.where(lane == t * unit_k + k, unit_experts[t, k], picks)
    for t in range(tasks):
        group = (lane >= t * unit_k) & (lane < (t + 1) * unit_k)
        for e in range(experts):
            weight = jnp.sum(jnp.where(group & (picks == e), probs, 0.0), axis=1, keepdims=True)
            mix_w[t, e] = jnp.broadcast_to(weight, mix_w.shape[2:])

    def relay(i):
        k = lax.rem(chip + chips - 1 - i, chips)
        block_copy(k * tile_size + c, me, c_send.at[k]).wait_recv()
        for j in range(1, tile_size):
            forward(k, j).start()

    loop(chips - 1, relay)

    for move in moves[4:11]:
        move.wait()

    def late(i):
        k = lax.rem(chip + chips - i, chips)
        for j in range(1, tile_size):
            q = k * tile_size + lax.rem(c + j, tile_size)
            block_copy(q, me, c_send.at[k]).wait_recv()

    loop(chips, late)

    rows = planes * plane_rows
    block = min(128, rows)
    tn = min(512, hid)
    per_block = block // own

    def row_block(b):
        r0 = pl.multiple_of(b * block, block)
        acc[...] = jnp.zeros_like(acc)

        def unit_block(n):
            n0 = pl.multiple_of(n * tn, tn)
            h = jnp.dot(
                rows_all[pl.ds(r0, block), :], up_v[:, pl.ds(n0, tn)], preferred_element_type=F32
            )
            h = jnp.maximum(h + up_b[:, pl.ds(pl.multiple_of(hid_base + n0, 128), tn)], 0.0)
            acc[...] += jnp.dot(
                h.astype(BF16), down_v[pl.ds(n0, tn), :], preferred_element_type=F32
            )

        loop(hid // tn, unit_block)
        sent[pl.ds(b * per_block, per_block)] = (
            acc[...].reshape(per_block, own, out_w).astype(BF16)
        )

    loop(rows // block, row_block)

    def term_copy(src, to):
        return pltpu.make_async_remote_copy(
            src_ref=sent.at[to],
            dst_ref=parts.at[src],
            send_sem=e_send.at[to],
            recv_sem=e_recv.at[src],
            device_id=rank_id(to),
            device_id_type=MESH,
        )

    def other_rank(i):
        return lax.rem(me + 1 + i, ranks)

    loop(ranks - 1, lambda i: term_copy(me, other_rank(i)).start())
    parts[me] = sent[me]
    for move in moves[11:]:
        move.wait()
    loop(ranks - 1, lambda i: term_copy(other_rank(i), me).wait_recv())

    def mix_copy(src_spot, to, t):
        return pltpu.make_async_remote_copy(
            src_ref=mixed.at[src_spot, t],
            dst_ref=mixed.at[src_spot, t],
            send_sem=m_send.at[t, to],
            recv_sem=m_recv.at[t, src_spot],
            device_id=plane_id(to),
            device_id_type=MESH,
        )

    per_expert = ranks // experts
    for t in range(tasks):
        total = jnp.zeros((own, out_w), F32)
        for e in range(experts):
            value = jnp.broadcast_to(down_b[pl.ds(e, 1), :], (own, out_w))
            if per_expert <= 2:
                for i in range(per_expert):
                    value = value + parts[e * per_expert + i].astype(F32)
            else:
                value = lax.fori_loop(
                    0,
                    per_expert,
                    lambda i, v, e=e: v + parts[e * per_expert + i].astype(F32),
                    value,
                )
            weight = mix_w[t, e]
            total = total + jnp.concatenate([weight] * (out_w // weight.shape[1]), axis=1) * value
        mixed[spot, t] = total.astype(BF16)
        loop(plane_devs - 1, lambda i, t=t: mix_copy(spot, other(i), t).start())

    def tower_copy(src_spot, to, t):
        return pltpu.make_async_remote_copy(
            src_ref=tower_send.at[t, to],
            dst_ref=tower_recv.at[t, src_spot],
            send_sem=t_send.at[t, to],
            recv_sem=t_recv.at[t, src_spot],
            device_id=plane_id(to),
            device_id_type=MESH,
        )

    for t in range(tasks):
        loop(plane_devs - 1, lambda i, t=t: mix_copy(other(i), spot, t).wait_recv())
        m = mixed[:, t].astype(F32).reshape(plane_rows, out_w).astype(BF16)
        h = jnp.dot(m, tin_v[t], preferred_element_type=F32) + tin_b[pl.ds(t, 1), :]
        h = jnp.maximum(h, 0.0).astype(BF16)
        y = jnp.dot(h, tout_v[t], preferred_element_type=F32)
        y = y.reshape(plane_devs, own, out_w)
        tower_own[t] = y
        tower_send[t] = y.astype(BF16)
        loop(plane_devs - 1, lambda i, t=t: tower_copy(spot, other(i), t).start())

    position = lax.broadcasted_iota(jnp.int32, (own, out_w), 0)
    for t in range(tasks):
        loop(plane_devs - 1, lambda i, t=t: tower_copy(other(i), spot, t).wait_recv())
        tower_recv[t, spot] = jnp.zeros((own, out_w), BF16)
        value = tower_own[t, spot] + jnp.sum(tower_recv[t].astype(F32), axis=0)
        value = value + tout_b[pl.ds(t, 1), :]
        out[t] = jnp.where(position < task_counts[0, t], value, 0.0).astype(BF16)

    loop(plane_devs - 1, lambda i: row_copy(spot, other(i)).wait_send())
    loop(chips - 1, lambda i: chip_send(i).wait_send())

    def relayed(i):
        for j in range(1, tile_size):
            forward(lax.rem(chip + i, chips), j).wait_send()

    loop(chips, relayed)
    loop(ranks - 1, lambda i: term_copy(me, other_rank(i)).wait_send())
    for t in range(tasks):
        loop(plane_devs - 1, lambda i, t=t: mix_copy(spot, other(i), t).wait_send())
        loop(plane_devs - 1, lambda i, t=t: tower_copy(spot, other(i), t).wait_send())


def solution(mesh):
    shape = mesh.shape
    planes, dp_size, tile_size = shape["expert"], shape["dp"], shape["tile"]

    def body(*args):
        (features, cross_weight, cross_bias, gate_weight, unit_experts, up_weight, up_bias,
         down_weight, down_bias, task_counts, tower_in, tower_in_bias, tower_out,
         tower_out_bias) = args
        plane_devs = dp_size * tile_size
        chips = planes * dp_size
        ranks = chips * tile_size
        own, width = features.shape
        tasks = unit_experts.shape[0]
        experts, out_w = down_bias.shape
        hid = up_weight.shape[1] // tile_size
        assert EXPERT_FF % hid == 0
        rows = ranks * own
        dma = pltpu.SemaphoreType.DMA
        vmem = pltpu.VMEM
        hbm = pl.BlockSpec(memory_space=pltpu.MemorySpace.HBM)
        smem = pl.BlockSpec(memory_space=pltpu.MemorySpace.SMEM)
        in_specs = [hbm] * 14
        in_specs[4] = smem
        in_specs[9] = smem
        result = pl.pallas_call(
            functools.partial(kernel, (planes, dp_size, tile_size)),
            out_shape=jax.ShapeDtypeStruct((tasks, own, out_w), BF16),
            in_specs=in_specs,
            out_specs=pl.BlockSpec(memory_space=pltpu.VMEM),
            scratch_shapes=[
                vmem((plane_devs, own, width), BF16),
                vmem(cross_weight.shape, BF16),
                vmem((1, width), F32),
                vmem(gate_weight.shape, BF16),
                vmem((width, hid), BF16),
                vmem((1, up_bias.shape[0]), F32),
                vmem((hid, out_w), BF16),
                vmem(down_bias.shape, F32),
                vmem(tower_in.shape, BF16),
                vmem(tower_in_bias.shape, F32),
                vmem(tower_out.shape, BF16),
                vmem(tower_out_bias.shape, F32),
                vmem((rows, width), BF16),
                vmem((min(128, rows), out_w), F32),
                vmem((ranks, own, out_w), BF16),
                vmem((ranks, own, out_w), BF16),
                vmem((tasks, experts, own, 128), F32),
                vmem((plane_devs, tasks, own, out_w), BF16),
                vmem((tasks, plane_devs, own, out_w), F32),
                vmem((tasks, plane_devs, own, out_w), BF16),
                vmem((tasks, plane_devs, own, out_w), BF16),
                dma((13,)),
                dma((plane_devs,)),
                dma((plane_devs,)),
                dma((chips,)),
                dma((chips, tile_size)),
                dma((ranks,)),
                dma((ranks,)),
                dma((ranks,)),
                dma((tasks, plane_devs)),
                dma((tasks, plane_devs)),
                dma((tasks, plane_devs)),
                dma((tasks, plane_devs)),
            ],
            compiler_params=pltpu.CompilerParams(
                collective_id=0, has_side_effects=True, vmem_limit_bytes=60 * 1024 * 1024
            ),
        )(
            features, cross_weight, cross_bias.reshape(1, -1), gate_weight, unit_experts,
            up_weight, up_bias.reshape(1, -1), down_weight, down_bias, task_counts, tower_in,
            tower_in_bias, tower_out, tower_out_bias,
        )
        return jnp.transpose(result, (1, 0, 2))

    return jax.shard_map(
        body,
        mesh=mesh,
        in_specs=(
            P(("groups", "expert", "dp", "tile"), None),
            P(None, ("dp", "tile")),
            P(),
            P(),
            P(),
            P(None, ("expert", "dp")),
            P(("expert", "dp")),
            P(("expert", "dp"), None),
            P(),
            P(("groups", "expert", "dp", "tile"), None),
            P(None, None, ("dp", "tile")),
            P(None, ("dp", "tile")),
            P(None, ("dp", "tile"), None),
            P(),
        ),
        out_specs=P(("groups", "expert", "dp", "tile"), None, None),
        check_vma=False,
    )
```
